32 devices in a mesh: section: 4 (over y, x), tile: 8 (over z, core).
Axes of the slice: x: 2, y: 2, z: 4, core: 2. Of those that a mesh axis runs over, the one named last changes fastest.
Arguments:
- hidden: bfloat16 [512, 2560], P('tile'), may hold values from -110 to 110
- keys_values: bfloat16 [4, 512, 2, 2560], P('section', 'tile'), may hold values from -60 to 60
- q_gain: float32 [4, 2560], P('section'), may hold values from 0.1 to 1.9
- tile_mask: int32 [8, 7], P('tile'), may hold values from 0 to 1, as said below
Outputs:
- attended: bfloat16 [4, 512, 2560], P('section', 'tile')
The draws below stay inside these ranges and needn't reach their ends.
Inputs may be any that keep to these rules, and one draw needn't show every extreme that they name: tile_mask[i, 3] is 1 for every tile; entries whose tile lies outside 0 to 7 are 0.
All inputs are finite; a program needn't handle non-finite values.
Results may differ from the reference program's by a relative error of at most 0.013.
Values may be sent and summed in bfloat16 or wider, within the bound.
No kernel may reach another device: no remote copies, remote signals or barrier semaphores. Data moves between devices by JAX's collectives and lax.ppermute only.
A program may use at most 64 MiB of HBM per device.

```python
import jax
import jax.numpy as jnp
from jax import lax

HEADS = 20
HD = 128
TOK_DEV = 64
WIN = 3
CH = 2560
LAYERS = 4
TILES = 8
TOKENS = 512


def draw_hidden(key, part):
    base = jnp.clip(jax.random.normal(jax.random.fold_in(key, 1), (TOKENS, CH), jnp.float32), -6.0, 6.0)
    return base.astype(jnp.bfloat16)


def draw_keys_values(key, part):
    key_part = jnp.clip(jax.random.normal(jax.random.fold_in(key, 11), (LAYERS, TOKENS, CH), jnp.float32), -6.0, 6.0)
    value_part = 3.0 * jnp.clip(jax.random.normal(jax.random.fold_in(key, 12), (LAYERS, TOKENS, CH), jnp.float32), -6.0, 6.0)
    return jnp.stack([key_part, value_part], axis=2).astype(jnp.bfloat16)


def draw_tile_mask(key, part):
    coins = jax.random.randint(key, (TILES, 2 * WIN + 1), 0, 5) < 3
    offsets = jnp.arange(2 * WIN + 1) - WIN
    target = jnp.arange(TILES)[:, None] + offsets[None, :]
    inside = (target >= 0) & (target < TILES)
    chosen = jnp.where(offsets[None, :] == 0, True, inside & coins)
    return jnp.where(chosen, 1, 0).astype(jnp.int32)


def setup_inputs(seed: int = 0) -> dict:
    arg_keys = jax.random.split(jax.random.key(seed), 5)
    return {
        "hidden": draw_hidden(jax.random.fold_in(arg_keys[4], 71), 0),
        "keys_values": draw_keys_values(jax.random.fold_in(arg_keys[4], 71), 0),
        "q_gain": jnp.clip(1.0 + 0.18 * jax.random.normal(arg_keys[2], (LAYERS, CH), jnp.float32), 0.1, 1.9),
        "tile_mask": draw_tile_mask(jax.random.fold_in(arg_keys[4], 71), 0),
    }


def attend(rows_in, gain_row, window, key_valid):
    floated = rows_in.astype(jnp.float32)
    mean_square = lax.optimization_barrier(jnp.mean(floated * floated, axis=-1, keepdims=True))
    query = (floated * lax.rsqrt(mean_square + 1e-06) * gain_row.astype(jnp.float32)).astype(jnp.bfloat16)
    row_count = rows_in.shape[0]
    key_count = window.shape[0]
    q_heads = query.reshape(row_count, HEADS, HD).astype(jnp.float32)
    k_heads = window[:, 0, :].reshape(key_count, HEADS, HD).astype(jnp.float32)
    v_heads = window[:, 1, :].reshape(key_count, HEADS, HD).astype(jnp.float32)
    scores = jnp.einsum('rhd,khd->hrk', q_heads, k_heads) * HD ** (-0.5)
    scores = jnp.where(key_valid[None, None, :], scores, -1e+30)
    row_max = lax.optimization_barrier(jnp.max(scores, axis=-1, keepdims=True))
    weights = jnp.exp(scores - row_max)
    denom = lax.optimization_barrier(jnp.sum(weights, axis=-1))
    weights_low = weights.astype(jnp.bfloat16)
    combined = jnp.einsum('hrk,khd->rhd', weights_low.astype(jnp.float32), v_heads)
    combined = combined / jnp.transpose(denom)[:, :, None]
    return combined.reshape(row_count, HEADS * HD).astype(jnp.bfloat16)

def reference(hidden, keys_values, q_gain, tile_mask):
    state = hidden
    outputs = []
    for layer in range(LAYERS):
        padded = jnp.pad(keys_values[layer], ((WIN * TOK_DEV, WIN * TOK_DEV), (0, 0), (0, 0)))

        def tile_fn(tile_no):
            row_start = (tile_no * TOK_DEV).astype(jnp.int32)
            rows_in = lax.dynamic_slice_in_dim(state, row_start, TOK_DEV, 0)
            window = lax.dynamic_slice_in_dim(padded, row_start, (2 * WIN + 1) * TOK_DEV, 0)
            mask_row = lax.dynamic_index_in_dim(tile_mask, tile_no.astype(jnp.int32), 0, keepdims=False)
            key_valid = jnp.repeat(mask_row > 0, TOK_DEV, total_repeat_length=(2 * WIN + 1) * TOK_DEV)
            return attend(rows_in, q_gain[layer], window, key_valid)
        result = lax.map(tile_fn, jnp.arange(TILES, dtype=jnp.int32)).reshape(TOKENS, CH)
        outputs.append(result)
        state = (state.astype(jnp.float32) + result.astype(jnp.float32)).astype(jnp.bfloat16)
    return jnp.stack(outputs, axis=0)
```

```python
import functools

import jax
import jax.numpy as jnp
from jax import lax
from jax.experimental import pallas as pl
from jax.experimental.pallas import tpu as pltpu
from jax.sharding import PartitionSpec as P

HD = 128
WIN = 3
NEG = -1e30
LOG2E = 1.4426950408889634
SLOTS = ((0, -2, 2, 1, -1, 3, -3), (0, -2, 2, -1, -3, 1, 3))
ATTEND_VMEM = 16 << 20
SPLIT_VMEM = 8 << 20


def vmem():
    return pl.BlockSpec(memory_space=pltpu.VMEM)


def smem():
    return pl.BlockSpec(memory_space=pltpu.SMEM)


def split_body(kv_ref, out_ref):
    rows = kv_ref.shape[0]
    i = lax.broadcasted_iota(jnp.int32, (2 * rows, 2 * rows), 0)
    j = lax.broadcasted_iota(jnp.int32, (2 * rows, 2 * rows), 1)
    source = jnp.where(i < rows, 2 * i, 2 * (i - rows) + 1)
    sort = jnp.where(j == source, 1.0, 0.0).astype(jnp.bfloat16)
    for c in range(0, kv_ref.shape[2], HD):
        mixed = kv_ref[:, :, c : c + HD].reshape(2 * rows, HD)
        both = jnp.dot(sort, mixed, preferred_element_type=jnp.float32).astype(jnp.bfloat16)
        out_ref[0, :, c : c + HD] = both[:rows]
        out_ref[1, :, c : c + HD] = both[rows:]


def split_keys_values(kv):
    rows, _, channels = kv.shape
    return pl.pallas_call(
        split_body,
        out_shape=jax.ShapeDtypeStruct((2, rows, channels), jnp.bfloat16),
        in_specs=[vmem()],
        out_specs=vmem(),
        compiler_params=pltpu.CompilerParams(vmem_limit_bytes=SPLIT_VMEM),
        name="split_kv",
    )(kv)


def attend_body(moment, has_next, mask_ref, src_ref, gain_ref, *refs):
    slots = len(SLOTS[0])
    tile_refs = refs[:slots]
    rest = list(refs[slots:])
    kept_ref = rest.pop(0) if moment else None
    out_ref = rest.pop(0)
    next_ref = rest.pop(0) if has_next else None
    rows, channels = src_ref.shape
    odd = lax.axis_index("tile") % 2
    live = lax.axis_index("section") == moment

    @pl.when(live)
    def _():
        x = src_ref[...].astype(jnp.float32)
        inv = lax.rsqrt(jnp.mean(x * x, axis=-1, keepdims=True) + 1e-06)
        lane = lax.broadcasted_iota(jnp.int32, (1, slots * rows), 1)
        bias = jnp.full((1, slots * rows), NEG, jnp.float32)
        for s in range(slots):
            bit = mask_ref[0, WIN + jnp.where(odd == 1, SLOTS[1][s], SLOTS[0][s])]
            here = (lane >= s * rows) & (lane < (s + 1) * rows) & (bit > 0)
            bias = jnp.where(here, 0.0, bias)
        for c in range(0, channels, HD):
            head = slice(c, c + HD)
            xh = src_ref[:, head].astype(jnp.float32)
            query = (xh * inv * gain_ref[:, head]).astype(jnp.bfloat16)
            keys = jnp.concatenate([t[0, :, head] for t in tile_refs], axis=0)
            values = jnp.concatenate([t[1, :, head] for t in tile_refs], axis=0)
            scores = lax.dot_general(
                query, keys, (((1,), (1,)), ((), ())), preferred_element_type=jnp.float32
            )
            scores = scores + bias
            top = jnp.max(scores, axis=-1, keepdims=True)
            weights = jnp.exp2((scores - top) * (HD**-0.5 * LOG2E))
            total = jnp.sum(weights, axis=-1, keepdims=True)
            mixed = jnp.dot(
                weights.astype(jnp.bfloat16), values, preferred_element_type=jnp.float32
            )
            result = (mixed / total).astype(jnp.bfloat16)
            out_ref[:, head] = result
            if has_next:
                next_ref[:, head] = (xh + result.astype(jnp.float32)).astype(jnp.bfloat16)

    if kept_ref is not None:

        @pl.when(jnp.logical_not(live))
        def _():
            out_ref[...] = kept_ref[...]


def attend(moment, has_next, mask, source, gain, tiles, kept):
    rows, channels = source.shape
    shape = jax.ShapeDtypeStruct((rows, channels), jnp.bfloat16)
    keys = len(tiles) * rows
    operands = [mask, source, gain, *tiles] + ([kept] if moment else [])
    outputs = 2 if has_next else 1
    return pl.pallas_call(
        functools.partial(attend_body, moment, has_next),
        out_shape=(shape,) * outputs,
        in_specs=[smem()] + [vmem()] * (len(operands) - 1),
        out_specs=(vmem(),) * outputs,
        compiler_params=pltpu.CompilerParams(vmem_limit_bytes=ATTEND_VMEM),
        cost_estimate=pl.CostEstimate(
            flops=4 * rows * keys * channels,
            bytes_accessed=4 * keys * channels + 6 * rows * channels,
            transcendentals=rows * keys * channels // HD,
        ),
        name="attend",
    )(*operands)


def exchange(own, tiles, parity):
    up = [(i, i + 2) for i in range(tiles - 2)]
    down = [(i + 2, i) for i in range(tiles - 2)]
    swap = [(i, i ^ 1) for i in range(tiles) if i ^ 1 < tiles]
    relay = [(i, i + 1) for i in range(1, tiles - 1, 2)] + [(i, i - 1) for i in range(2, tiles, 2)]
    below = lax.ppermute(own, "tile", up)
    above = lax.ppermute(own, "tile", down)
    partner = lax.ppermute(own, "tile", swap)
    far = lax.ppermute(jnp.where(parity == 1, below, above), "tile", relay)
    partner_below = lax.ppermute(below, "tile", swap)
    partner_above = lax.ppermute(above, "tile", swap)
    return [own, below, above, partner, partner_below, partner_above, far]


def on_device(hidden, keys_values, q_gain, tile_mask):
    sections = lax.axis_size("section")
    tiles = lax.axis_size("tile")
    parity = lax.axis_index("tile") % 2
    own = split_keys_values(keys_values[0])
    window = exchange(own, tiles, parity)
    source, attended = hidden, None
    for moment in range(sections):
        has_next = moment + 1 < sections
        results = attend(moment, has_next, tile_mask, source, q_gain, window, attended)
        attended = results[0]
        if has_next:
            hop = [(i, i + 1) for i in range(sections - 1)]
            source = lax.ppermute(results[1], "section", hop)
    return attended[None]


def solution(mesh):
    in_specs = (
        P("tile", None),
        P("section", "tile", None, None),
        P("section", None),
        P("tile", None),
    )
    out_specs = P("section", "tile", None)
    return jax.shard_map(
        on_device, mesh=mesh, in_specs=in_specs, out_specs=out_specs, check_vma=False
    )
```

```python
import functools

import jax
import jax.numpy as jnp
from jax import lax
from jax.experimental import pallas as pl
from jax.experimental.pallas import tpu as pltpu
from jax.sharding import PartitionSpec as P


HD = 128
WIN = 3
LANES = 128
NEG = -1e30
LOG2E = 1.4426950408889634
PIECES = 2
SLOTS = (0, 2, -2, -3, 1, -1, 3)
ATTEND_VMEM = 24 << 20
SPLIT_VMEM = 8 << 20


def vmem():
    return pl.BlockSpec(memory_space=pltpu.VMEM)


def smem():
    return pl.BlockSpec(memory_space=pltpu.SMEM)


def split_body(kv_ref, out_ref):
    rows = kv_ref.shape[0]
    i = lax.broadcasted_iota(jnp.int32, (2 * rows, 2 * rows), 0)
    j = lax.broadcasted_iota(jnp.int32, (2 * rows, 2 * rows), 1)
    source = jnp.where(i < rows, 2 * i, 2 * (i - rows) + 1)
    sort = jnp.where(j == source, 1.0, 0.0).astype(jnp.bfloat16)
    for c in range(0, kv_ref.shape[2], HD):
        mixed = kv_ref[:, :, c : c + HD].reshape(2 * rows, HD)
        both = jnp.dot(sort, mixed, preferred_element_type=jnp.float32).astype(jnp.bfloat16)
        out_ref[0, :, c : c + HD] = both[:rows]
        out_ref[1, :, c : c + HD] = both[rows:]


def split_keys_values(kv):
    rows, _, channels = kv.shape
    return pl.pallas_call(
        split_body,
        out_shape=jax.ShapeDtypeStruct((2, rows, channels), jnp.bfloat16),
        in_specs=[vmem()],
        out_specs=vmem(),
        compiler_params=pltpu.CompilerParams(vmem_limit_bytes=SPLIT_VMEM),
        name="split_kv",
    )(kv)


def attend_rows(mask_ref, src_ref, rows, gain_ref, tile_refs):
    count = rows.stop - rows.start
    channels = src_ref.shape[1]
    tile_rows = tile_refs[0].shape[1]
    keys = len(tile_refs) * tile_rows
    heads = LANES // count
    width = heads * HD
    sign = 1 - 2 * (lax.axis_index("tile") % 2)
    x = src_ref[rows, :].astype(jnp.float32)
    inv = lax.rsqrt(jnp.mean(x * x, axis=-1, keepdims=True) + 1e-06)
    key = lax.broadcasted_iota(jnp.int32, (keys, LANES), 0)
    bias = jnp.full((keys, LANES), NEG, jnp.float32)
    for s, offset in enumerate(SLOTS):
        bit = mask_ref[0, WIN + sign * offset]
        here = (key >= s * tile_rows) & (key < (s + 1) * tile_rows) & (bit > 0)
        bias = jnp.where(here, 0.0, bias)
    zero = jnp.zeros((count, HD), jnp.bfloat16)
    groups = [slice(c, c + width) for c in range(0, channels, width)]
    states = [src_ref[rows, g].astype(jnp.float32) for g in groups]
    queries = []
    for g, state in zip(groups, states):
        query = (state * inv * gain_ref[:, g]).astype(jnp.bfloat16)
        blocks = [
            jnp.concatenate(
                [query[:, b * HD : (b + 1) * HD] if a == b else zero for b in range(heads)], axis=1
            )
            for a in range(heads)
        ]
        queries.append(jnp.concatenate(blocks, axis=0))
    scores = [
        lax.dot_general(
            jnp.concatenate([t[0, :, g] for t in tile_refs], axis=0),
            query,
            (((1,), (1,)), ((), ())),
            preferred_element_type=jnp.float32,
        )
        + bias
        for g, query in zip(groups, queries)
    ]
    tops = [jnp.max(s, axis=0, keepdims=True) for s in scores]
    weights = [jnp.exp2((s - top) * (HD**-0.5 * LOG2E)) for s, top in zip(scores, tops)]
    totals = [jnp.sum(w, axis=0, keepdims=True) for w in weights]
    mixed = [
        lax.dot_general(
            w.astype(jnp.bfloat16),
            jnp.concatenate([t[1, :, g] for t in tile_refs], axis=0),
            (((0,), (0,)), ((), ())),
            preferred_element_type=jnp.float32,
        )
        for g, w in zip(groups, weights)
    ]
    done = []
    for g, state, m, total in zip(groups, states, mixed, totals):
        by_row = jnp.transpose(jnp.broadcast_to(total, (LANES, LANES)))
        result = jnp.concatenate(
            [
                m[b * count : (b + 1) * count, b * HD : (b + 1) * HD]
                / by_row[b * count : (b + 1) * count]
                for b in range(heads)
            ],
            axis=1,
        ).astype(jnp.bfloat16)
        done.append((g, state, result))
    return done


def attend_body(moment, has_next, rows, mask_ref, src_ref, gain_ref, *refs):
    tile_refs = refs[: len(SLOTS)]
    rest = list(refs[len(SLOTS) :])
    kept_ref = rest.pop(0) if moment else None
    out_ref = rest.pop(0)
    next_ref = rest.pop(0) if has_next else None
    live = lax.axis_index("section") == moment

    @pl.when(live)
    def _():
        for g, state, result in attend_rows(mask_ref, src_ref, rows, gain_ref, tile_refs):
            out_ref[:, g] = result
            if has_next:
                next_ref[:, g] = (state + result.astype(jnp.float32)).astype(jnp.bfloat16)

    if kept_ref is not None:

        @pl.when(jnp.logical_not(live))
        def _():
            out_ref[...] = kept_ref[...]


def attend(moment, has_next, rows, mask, source, gain, tiles, kept):
    count = rows.stop - rows.start
    channels = source.shape[1]
    shape = jax.ShapeDtypeStruct((count, channels), jnp.bfloat16)
    keys = len(tiles) * tiles[0].shape[1]
    operands = [mask, source, gain, *tiles] + ([kept] if moment else [])
    outputs = 2 if has_next else 1
    return pl.pallas_call(
        functools.partial(attend_body, moment, has_next, rows),
        out_shape=(shape,) * outputs,
        in_specs=[smem()] + [vmem()] * (len(operands) - 1),
        out_specs=(vmem(),) * outputs,
        compiler_params=pltpu.CompilerParams(vmem_limit_bytes=ATTEND_VMEM),
        cost_estimate=pl.CostEstimate(
            flops=4 * count * keys * channels,
            bytes_accessed=4 * keys * channels + 6 * count * channels,
            transcendentals=count * keys * channels // HD,
        ),
        name="attend",
    )(*operands)


def exchange(own, tiles):
    odd = range(1, tiles, 2)
    even = range(0, tiles, 2)

    def inside(pairs):
        return [(i, j) for i, j in pairs if 0 <= j < tiles]

    def move(tile, pairs):
        return lax.ppermute(tile, "tile", pairs)

    swap = inside([(i, i ^ 1) for i in range(tiles)])
    relay = inside([(i, i + 1) for i in odd] + [(i, i - 1) for i in even])
    outward = inside([(i, i + 2) for i in odd] + [(i, i - 2) for i in even])
    first = move(own, outward)
    partner = move(own, swap)
    second = move(own, [(j, i) for i, j in outward])
    far = move(first, relay)
    partner_first = move(first, swap)
    partner_second = move(second, swap)
    return [own, first, second, far, partner, partner_first, partner_second]


def on_device(hidden, keys_values, q_gain, tile_mask):
    sections = lax.axis_size("section")
    rows = hidden.shape[0]
    count = rows // PIECES
    own = split_keys_values(keys_values[0])
    window = exchange(own, lax.axis_size("tile"))
    sources = [(hidden, slice(p * count, (p + 1) * count)) for p in range(PIECES)]
    kept = [None] * PIECES
    for moment in range(sections):
        has_next = moment + 1 < sections
        for p, (source, span) in enumerate(sources):
            results = attend(moment, has_next, span, tile_mask, source, q_gain, window, kept[p])
            kept[p] = results[0]
            if has_next:
                arrived = lax.ppermute(results[1], "section", [(moment, moment + 1)])
                sources[p] = (arrived, slice(0, count))
    attended = kept[0] if PIECES == 1 else jnp.concatenate(kept, axis=0)
    return attended[None]


def solution(mesh):
    in_specs = (
        P("tile", None),
        P("section", "tile", None, None),
        P("section", None),
        P("tile", None),
    )
    out_specs = P("section", "tile", None)
    return jax.shard_map(
        on_device, mesh=mesh, in_specs=in_specs, out_specs=out_specs, check_vma=False
    )
```

```python
import functools

import jax
import jax.numpy as jnp
from jax import lax
from jax.experimental import pallas as pl
from jax.experimental.pallas import tpu as pltpu
from jax.sharding import PartitionSpec as P


HD = 128
WIN = 3
LANES = 128
NEG = -1e30
LOG2E = 1.4426950408889634
PIECES = 2
SLOTS = (0, 2, -2, -3, 1, -1, 3)
ATTEND_VMEM = 24 << 20
SPLIT_VMEM = 8 << 20


def vmem():
    return pl.BlockSpec(memory_space=pltpu.VMEM)


def smem():
    return pl.BlockSpec(memory_space=pltpu.SMEM)


def split_body(kv_ref, out_ref):
    rows = kv_ref.shape[0]
    i = lax.broadcasted_iota(jnp.int32, (2 * rows, 2 * rows), 0)
    j = lax.broadcasted_iota(jnp.int32, (2 * rows, 2 * rows), 1)
    source = jnp.where(i < rows, 2 * i, 2 * (i - rows) + 1)
    sort = jnp.where(j == source, 1.0, 0.0).astype(jnp.bfloat16)
    for c in range(0, kv_ref.shape[2], HD):
        mixed = kv_ref[:, :, c : c + HD].reshape(2 * rows, HD)
        both = jnp.dot(sort, mixed, preferred_element_type=jnp.float32).astype(jnp.bfloat16)
        out_ref[0, :, c : c + HD] = both[:rows]
        out_ref[1, :, c : c + HD] = both[rows:]


def split_keys_values(kv):
    rows, _, channels = kv.shape
    return pl.pallas_call(
        split_body,
        out_shape=jax.ShapeDtypeStruct((2, rows, channels), jnp.bfloat16),
        in_specs=[vmem()],
        out_specs=vmem(),
        compiler_params=pltpu.CompilerParams(vmem_limit_bytes=SPLIT_VMEM),
        name="split_kv",
    )(kv)


def bias_body(tile_rows, mask_ref, out_ref):
    sign = 1 - 2 * (lax.axis_index("tile") % 2)
    for s, offset in enumerate(SLOTS):
        bit = mask_ref[0, WIN + sign * offset]
        block = jnp.full((tile_rows, LANES), jnp.where(bit > 0, 0.0, NEG), jnp.float32)
        out_ref[s * tile_rows : (s + 1) * tile_rows, :] = block


def mask_bias(mask, tile_rows):
    return pl.pallas_call(
        functools.partial(bias_body, tile_rows),
        out_shape=jax.ShapeDtypeStruct((len(SLOTS) * tile_rows, LANES), jnp.float32),
        in_specs=[smem()],
        out_specs=vmem(),
        compiler_params=pltpu.CompilerParams(vmem_limit_bytes=SPLIT_VMEM),
        name="mask_bias",
    )(mask)


def attend_rows(bias_ref, src_ref, rows, gain_ref, tile_refs):
    count = rows.stop - rows.start
    channels = src_ref.shape[1]
    width = LANES // count * HD
    x = src_ref[rows, :].astype(jnp.float32)
    inv = lax.rsqrt(jnp.mean(x * x, axis=-1, keepdims=True) + 1e-06)
    zero = jnp.zeros((count, HD), jnp.bfloat16)
    groups = [slice(c, min(c + width, channels)) for c in range(0, channels, width)]
    sizes = [(g.stop - g.start) // HD for g in groups]
    states = [src_ref[rows, g].astype(jnp.float32) for g in groups]
    queries = []
    for g, heads, state in zip(groups, sizes, states):
        query = (state * inv * gain_ref[:, g]).astype(jnp.bfloat16)
        blocks = [
            jnp.concatenate(
                [query[:, b * HD : (b + 1) * HD] if a == b else zero for b in range(heads)], axis=1
            )
            for a in range(heads)
        ]
        queries.append(jnp.concatenate(blocks, axis=0))
    scores = [
        lax.dot_general(
            jnp.concatenate([t[0, :, g] for t in tile_refs], axis=0),
            query,
            (((1,), (1,)), ((), ())),
            preferred_element_type=jnp.float32,
        )
        + bias_ref[:, : heads * count]
        for g, heads, query in zip(groups, sizes, queries)
    ]
    tops = [jnp.max(s, axis=0, keepdims=True) for s in scores]
    weights = [jnp.exp2((s - top) * (HD**-0.5 * LOG2E)) for s, top in zip(scores, tops)]
    totals = [jnp.sum(w, axis=0, keepdims=True) for w in weights]
    mixed = [
        lax.dot_general(
            w.astype(jnp.bfloat16),
            jnp.concatenate([t[1, :, g] for t in tile_refs], axis=0),
            (((0,), (0,)), ((), ())),
            preferred_element_type=jnp.float32,
        )
        for g, w in zip(groups, weights)
    ]
    done = []
    for g, heads, state, m, total in zip(groups, sizes, states, mixed, totals):
        by_row = jnp.transpose(jnp.broadcast_to(total, (HD, heads * count)))
        result = jnp.concatenate(
            [
                m[b * count : (b + 1) * count, b * HD : (b + 1) * HD]
                / by_row[b * count : (b + 1) * count]
                for b in range(heads)
            ],
            axis=1,
        ).astype(jnp.bfloat16)
        done.append((g, state, result))
    return done


def attend_body(moment, has_next, rows, joined, bias_ref, src_ref, gain_ref, *refs):
    tile_refs = refs[: len(SLOTS)]
    rest = list(refs[len(SLOTS) :])
    kept_ref = rest.pop(0) if moment else None
    earlier_refs = [rest.pop(0) for _ in range(joined)]
    out_ref = rest.pop(0)
    next_ref = rest.pop(0) if has_next else None
    live = lax.axis_index("section") == moment
    at = 0
    for ref in earlier_refs:
        out_ref[at : at + ref.shape[0], :] = ref[...]
        at += ref.shape[0]
    span = slice(at, at + rows.stop - rows.start)

    @pl.when(live)
    def _():
        for g, state, result in attend_rows(bias_ref, src_ref, rows, gain_ref, tile_refs):
            out_ref[span, g] = result
            if has_next:
                next_ref[:, g] = (state + result.astype(jnp.float32)).astype(jnp.bfloat16)

    if kept_ref is not None:

        @pl.when(jnp.logical_not(live))
        def _():
            out_ref[span, :] = kept_ref[...]


def attend(moment, has_next, rows, bias, source, gain, tiles, kept, earlier=()):
    count = rows.stop - rows.start
    channels = source.shape[1]
    keys = len(tiles) * tiles[0].shape[1]
    operands = [bias, source, gain, *tiles] + ([kept] if moment else []) + list(earlier)
    total = count + sum(e.shape[0] for e in earlier)
    shapes = [jax.ShapeDtypeStruct((total, channels), jnp.bfloat16)]
    if has_next:
        shapes.append(jax.ShapeDtypeStruct((count, channels), jnp.bfloat16))
    return pl.pallas_call(
        functools.partial(attend_body, moment, has_next, rows, len(earlier)),
        out_shape=tuple(shapes),
        in_specs=[vmem()] * len(operands),
        out_specs=(vmem(),) * len(shapes),
        compiler_params=pltpu.CompilerParams(vmem_limit_bytes=ATTEND_VMEM),
        cost_estimate=pl.CostEstimate(
            flops=4 * count * keys * channels,
            bytes_accessed=4 * keys * channels + 6 * count * channels,
            transcendentals=count * keys * channels // HD,
        ),
        name="attend",
    )(*operands)


def exchange(own, tiles):
    odd = range(1, tiles, 2)
    even = range(0, tiles, 2)

    def inside(pairs):
        return [(i, j) for i, j in pairs if 0 <= j < tiles]

    def move(tile, pairs):
        return lax.ppermute(tile, "tile", pairs)

    swap = inside([(i, i ^ 1) for i in range(tiles)])
    relay = inside([(i, i + 1) for i in odd] + [(i, i - 1) for i in even])
    outward = inside([(i, i + 2) for i in odd] + [(i, i - 2) for i in even])
    first = move(own, outward)
    partner = move(own, swap)
    second = move(own, [(j, i) for i, j in outward])
    far = move(first, relay)
    partner_first = move(first, swap)
    partner_second = move(second, swap)
    return [own, first, second, far, partner, partner_first, partner_second]


def on_device(hidden, keys_values, q_gain, tile_mask):
    sections = lax.axis_size("section")
    rows = hidden.shape[0]
    count = rows // PIECES
    own = split_keys_values(keys_values[0])
    bias = mask_bias(tile_mask, rows)
    window = exchange(own, lax.axis_size("tile"))
    sources = [(hidden, slice(p * count, (p + 1) * count)) for p in range(PIECES)]
    kept = [None] * PIECES
    for moment in range(sections):
        has_next = moment + 1 < sections
        for p, (source, span) in enumerate(sources):
            earlier = kept[:p] if not has_next and p + 1 == PIECES else ()
            results = attend(
                moment, has_next, span, bias, source, q_gain, window, kept[p], earlier
            )
            kept[p] = results[0]
            if has_next:
                arrived = lax.ppermute(results[1], "section", [(moment, moment + 1)])
                sources[p] = (arrived, slice(0, count))
    return kept[-1][None]


def solution(mesh):
    in_specs = (
        P("tile", None),
        P("section", "tile", None, None),
        P("section", None),
        P("tile", None),
    )
    out_specs = P("section", "tile", None)
    return jax.shard_map(
        on_device, mesh=mesh, in_specs=in_specs, out_specs=out_specs, check_vma=False
    )
```

```python
import functools

import jax
import jax.numpy as jnp
from jax import lax
from jax.experimental import pallas as pl
from jax.experimental.pallas import tpu as pltpu
from jax.sharding import PartitionSpec as P


HD = 128
WIN = 3
LANES = 128
NEG = -1e30
SCALE = HD**-0.5 * 1.4426950408889634
PIECES = 2
SLOTS = (0, 2, -2, -3, 1, -1, 3)
ATTEND_VMEM = 24 << 20
SPLIT_VMEM = 8 << 20


def vmem():
    return pl.BlockSpec(memory_space=pltpu.VMEM)


def smem():
    return pl.BlockSpec(memory_space=pltpu.SMEM)


def split_body(kv_ref, out_ref):
    rows = kv_ref.shape[0]
    i = lax.broadcasted_iota(jnp.int32, (2 * rows, 2 * rows), 0)
    j = lax.broadcasted_iota(jnp.int32, (2 * rows, 2 * rows), 1)
    source = jnp.where(i < rows, 2 * i, 2 * (i - rows) + 1)
    sort = jnp.where(j == source, 1.0, 0.0).astype(jnp.bfloat16)
    for c in range(0, kv_ref.shape[2], HD):
        mixed = kv_ref[:, :, c : c + HD].reshape(2 * rows, HD)
        both = jnp.dot(sort, mixed, preferred_element_type=jnp.float32).astype(jnp.bfloat16)
        out_ref[0, :, c : c + HD] = both[:rows]
        out_ref[1, :, c : c + HD] = both[rows:]


def split_keys_values(kv):
    rows, _, channels = kv.shape
    return pl.pallas_call(
        split_body,
        out_shape=jax.ShapeDtypeStruct((2, rows, channels), jnp.bfloat16),
        in_specs=[vmem()],
        out_specs=vmem(),
        compiler_params=pltpu.CompilerParams(vmem_limit_bytes=SPLIT_VMEM),
        name="split_kv",
    )(kv)


def bias_body(tile_rows, mask_ref, out_ref):
    sign = 1 - 2 * (lax.axis_index("tile") % 2)
    for s, offset in enumerate(SLOTS):
        bit = mask_ref[0, WIN + sign * offset]
        block = jnp.full((tile_rows, LANES), jnp.where(bit > 0, 0.0, NEG), jnp.float32)
        out_ref[s * tile_rows : (s + 1) * tile_rows, :] = block


def mask_bias(mask, tile_rows):
    return pl.pallas_call(
        functools.partial(bias_body, tile_rows),
        out_shape=jax.ShapeDtypeStruct((len(SLOTS) * tile_rows, LANES), jnp.float32),
        in_specs=[smem()],
        out_specs=vmem(),
        compiler_params=pltpu.CompilerParams(vmem_limit_bytes=SPLIT_VMEM),
        name="mask_bias",
    )(mask)


def head_groups(count, channels):
    width = LANES // count * HD
    groups = [slice(c, min(c + width, channels)) for c in range(0, channels, width)]
    return groups, [(g.stop - g.start) // HD for g in groups]


def per_row(lanes, heads, count):
    return jnp.transpose(jnp.broadcast_to(lanes, (HD, heads * count)))


def attend_tiles(bias, src_ref, rows, gain_ref, tile_refs):
    count = rows.stop - rows.start
    groups, sizes = head_groups(count, src_ref.shape[1])
    x = src_ref[rows, :].astype(jnp.float32)
    inv = lax.rsqrt(jnp.mean(x * x, axis=-1, keepdims=True) + 1e-06)
    zero = jnp.zeros((count, HD), jnp.bfloat16)
    states = [src_ref[rows, g].astype(jnp.float32) for g in groups]
    queries = []
    for g, heads, state in zip(groups, sizes, states):
        query = (state * inv * gain_ref[:, g]).astype(jnp.bfloat16)
        blocks = [
            jnp.concatenate(
                [query[:, b * HD : (b + 1) * HD] if a == b else zero for b in range(heads)], axis=1
            )
            for a in range(heads)
        ]
        queries.append(jnp.concatenate(blocks, axis=0))
    scores = [
        lax.dot_general(
            jnp.concatenate([t[0, :, g] for t in tile_refs], axis=0),
            query,
            (((1,), (1,)), ((), ())),
            preferred_element_type=jnp.float32,
        )
        + bias[:, : heads * count]
        for g, heads, query in zip(groups, sizes, queries)
    ]
    tops = [jnp.max(s, axis=0, keepdims=True) for s in scores]

    def weigh(tops):
        weights = [jnp.exp2((s - top) * SCALE) for s, top in zip(scores, tops)]
        totals = [jnp.sum(w, axis=0, keepdims=True) for w in weights]
        mixed = [
            lax.dot_general(
                w.astype(jnp.bfloat16),
                jnp.concatenate([t[1, :, g] for t in tile_refs], axis=0),
                (((0,), (0,)), ((), ())),
                preferred_element_type=jnp.float32,
            )
            for g, w in zip(groups, weights)
        ]
        blocks = [
            [m[b * count : (b + 1) * count, b * HD : (b + 1) * HD] for b in range(heads)]
            for m, heads in zip(mixed, sizes)
        ]
        return totals, blocks

    return states, tops, weigh


def attend_rows(bias_ref, src_ref, rows, gain_ref, tile_refs):
    count = rows.stop - rows.start
    groups, sizes = head_groups(count, src_ref.shape[1])
    states, tops, weigh = attend_tiles(bias_ref[...], src_ref, rows, gain_ref, tile_refs)
    totals, mixed = weigh(tops)
    done = []
    for g, heads, state, blocks, total in zip(groups, sizes, states, mixed, totals):
        by_row = per_row(total, heads, count)
        parts = [m / by_row[b * count : (b + 1) * count] for b, m in enumerate(blocks)]
        done.append((g, state, jnp.concatenate(parts, axis=1).astype(jnp.bfloat16)))
    return done


def partial_body(slots, carried, last, bias_ref, src_ref, gain_ref, *refs):
    tile_refs = refs[: len(slots)]
    refs = refs[len(slots) :]
    top_in, total_in, sum_in = refs[:3] if carried else (None,) * 3
    refs = refs[3:] if carried else refs
    rows, channels = src_ref.shape
    tile_rows = tile_refs[0].shape[1]
    groups, sizes = head_groups(rows, channels)

    @pl.when(lax.axis_index("section") == 0)
    def _():
        bias = jnp.concatenate(
            [bias_ref[s * tile_rows : (s + 1) * tile_rows, :] for s in slots], axis=0
        )
        states, tops, weigh = attend_tiles(bias, src_ref, slice(0, rows), gain_ref, tile_refs)
        if carried:
            tops = [jnp.maximum(t, top_in[n : n + 1, :]) for n, t in enumerate(tops)]
        totals, sums = weigh(tops)
        for n, (g, heads) in enumerate(zip(groups, sizes)):
            total, blocks = totals[n], sums[n]
            if carried:
                fade = jnp.exp2((top_in[n : n + 1, :] - tops[n]) * SCALE)
                total = total + fade * total_in[n : n + 1, :]
                by_row = per_row(fade, heads, rows)
                blocks = [
                    m
                    + by_row[b * rows : (b + 1) * rows]
                    * sum_in[:, g.start + b * HD : g.start + (b + 1) * HD]
                    for b, m in enumerate(blocks)
                ]
            if not last:
                top_out, total_out, sum_out = refs
                top_out[n : n + 1, :] = tops[n]
                total_out[n : n + 1, :] = total
                for b, m in enumerate(blocks):
                    sum_out[:, g.start + b * HD : g.start + (b + 1) * HD] = m
                continue
            by_row = per_row(total, heads, rows)
            parts = [m / by_row[b * rows : (b + 1) * rows] for b, m in enumerate(blocks)]
            result = jnp.concatenate(parts, axis=1).astype(jnp.bfloat16)
            state = (states[n] + result.astype(jnp.float32)).astype(jnp.bfloat16)
            count = rows // PIECES
            for p in range(PIECES):
                span = slice(p * count, (p + 1) * count)
                refs[p][:, g] = result[span]
                refs[PIECES + p][:, g] = state[span]


def partial_attend(slots, last, bias, source, gain, tiles, carry=()):
    rows, channels = source.shape
    if last:
        piece = jax.ShapeDtypeStruct((rows // PIECES, channels), jnp.bfloat16)
        shapes = (piece,) * (2 * PIECES)
    else:
        lanes = jax.ShapeDtypeStruct((len(head_groups(rows, channels)[0]), LANES), jnp.float32)
        shapes = (lanes, lanes, jax.ShapeDtypeStruct((rows, channels), jnp.float32))
    operands = [bias, source, gain, *tiles, *carry]
    keys = len(tiles) * rows
    return pl.pallas_call(
        functools.partial(partial_body, slots, bool(carry), last),
        out_shape=shapes,
        in_specs=[vmem()] * len(operands),
        out_specs=(vmem(),) * len(shapes),
        compiler_params=pltpu.CompilerParams(vmem_limit_bytes=ATTEND_VMEM),
        cost_estimate=pl.CostEstimate(
            flops=4 * rows * keys * channels,
            bytes_accessed=4 * keys * channels + 6 * rows * channels,
            transcendentals=rows * keys * channels // HD,
        ),
        name="partial_attend",
    )(*operands)


def attend_body(moment, has_next, joined, bias_ref, src_ref, gain_ref, *refs):
    tile_refs = refs[: len(SLOTS)]
    rest = list(refs[len(SLOTS) :])
    kept_ref = rest.pop(0)
    earlier_refs = [rest.pop(0) for _ in range(joined)]
    out_ref = rest.pop(0)
    next_ref = rest.pop(0) if has_next else None
    live = lax.axis_index("section") == moment
    at = 0
    for ref in earlier_refs:
        out_ref[at : at + ref.shape[0], :] = ref[...]
        at += ref.shape[0]
    rows = src_ref.shape[0]
    span = slice(at, at + rows)

    @pl.when(live)
    def _():
        for g, state, result in attend_rows(bias_ref, src_ref, slice(0, rows), gain_ref, tile_refs):
            out_ref[span, g] = result
            if has_next:
                next_ref[:, g] = (state + result.astype(jnp.float32)).astype(jnp.bfloat16)

    @pl.when(jnp.logical_not(live))
    def _():
        out_ref[span, :] = kept_ref[...]


def attend(moment, has_next, bias, source, gain, tiles, kept, earlier):
    count, channels = source.shape
    keys = len(tiles) * tiles[0].shape[1]
    operands = [bias, source, gain, *tiles, kept, *earlier]
    total = count + sum(e.shape[0] for e in earlier)
    shapes = [jax.ShapeDtypeStruct((total, channels), jnp.bfloat16)]
    if has_next:
        shapes.append(jax.ShapeDtypeStruct((count, channels), jnp.bfloat16))
    return pl.pallas_call(
        functools.partial(attend_body, moment, has_next, len(earlier)),
        out_shape=tuple(shapes),
        in_specs=[vmem()] * len(operands),
        out_specs=(vmem(),) * len(shapes),
        compiler_params=pltpu.CompilerParams(vmem_limit_bytes=ATTEND_VMEM),
        cost_estimate=pl.CostEstimate(
            flops=4 * count * keys * channels,
            bytes_accessed=4 * keys * channels + 6 * count * channels,
            transcendentals=count * keys * channels // HD,
        ),
        name="attend",
    )(*operands)


def first_layer(raw, own, tiles, bias, hidden, gain):
    last = tiles - 1

    def move(tile, pairs):
        return lax.ppermute(tile, "tile", pairs)

    swap = [(i, i ^ 1) for i in range(tiles)]
    outward = [(0, 1), (last, last - 1)]
    outward += [(i, i + 2) for i in range(1, last, 2)] + [(i, i - 2) for i in range(2, tiles, 2)]
    relay = [(0, 0), (last, last)]
    relay += [(i, i + 1) for i in range(1, last, 2)] + [(i, i - 1) for i in range(2, tiles, 2)]
    first_raw = move(raw, outward)
    partner = move(own, swap)
    carry = partial_attend((0, 4), False, bias, hidden, gain, [own, partner])
    second = move(own, [(j, i) for i, j in outward])
    far_raw = move(first_raw, relay)
    first = split_keys_values(first_raw)
    partner_first = move(first, swap)
    partner_second = move(second, swap)
    tail = [first, second, partner_first, partner_second]
    carry = partial_attend((1, 2, 5, 6), False, bias, hidden, gain, tail, carry)
    far = split_keys_values(far_raw)
    pieces = partial_attend((3,), True, bias, hidden, gain, [far], carry)
    return [own, first, second, far, partner, partner_first, partner_second], pieces


def on_device(hidden, keys_values, q_gain, tile_mask):
    sections = lax.axis_size("section")
    rows = hidden.shape[0]
    raw = keys_values[0]
    own = split_keys_values(raw)
    bias = mask_bias(tile_mask, rows)
    window, pieces = first_layer(raw, own, lax.axis_size("tile"), bias, hidden, q_gain)
    kept, following = list(pieces[:PIECES]), list(pieces[PIECES:])
    for moment in range(1, sections):
        has_next = moment + 1 < sections
        others = [i for i in range(sections)[::-1] if i not in (moment - 1, moment)]
        cycle = [moment - 1, moment, *others]
        hop = list(zip(cycle, cycle[1:] + cycle[:1]))
        for p in range(PIECES):
            source = lax.ppermute(following[p], "section", hop)
            earlier = kept[:p] if not has_next and p + 1 == PIECES else ()
            results = attend(moment, has_next, bias, source, q_gain, window, kept[p], earlier)
            kept[p] = results[0]
            if has_next:
                following[p] = results[1]
    return kept[-1][None]


def solution(mesh):
    in_specs = (
        P("tile", None),
        P("section", "tile", None, None),
        P("section", None),
        P("tile", None),
    )
    out_specs = P("section", "tile", None)
    return jax.shard_map(
        on_device, mesh=mesh, in_specs=in_specs, out_specs=out_specs, check_vma=False
    )
```

```python
import functools

import jax
import jax.numpy as jnp
from jax import lax
from jax.experimental import pallas as pl
from jax.experimental.pallas import tpu as pltpu
from jax.sharding import PartitionSpec as P


HD = 128
WIN = 3
LANES = 128
NEG = -1e30
SCALE = HD**-0.5 * 1.4426950408889634
PIECES = 4
SLOTS = (0, 2, -2, -3, 1, -1, 3)
ATTEND_VMEM = 24 << 20
SPLIT_VMEM = 8 << 20


def vmem():
    return pl.BlockSpec(memory_space=pltpu.VMEM)


def smem():
    return pl.BlockSpec(memory_space=pltpu.SMEM)


def split_body(kv_ref, out_ref):
    rows = kv_ref.shape[0]
    i = lax.broadcasted_iota(jnp.int32, (2 * rows, 2 * rows), 0)
    j = lax.broadcasted_iota(jnp.int32, (2 * rows, 2 * rows), 1)
    source = jnp.where(i < rows, 2 * i, 2 * (i - rows) + 1)
    sort = jnp.where(j == source, 1.0, 0.0).astype(jnp.bfloat16)
    for c in range(0, kv_ref.shape[2], HD):
        mixed = kv_ref[:, :, c : c + HD].reshape(2 * rows, HD)
        both = jnp.dot(sort, mixed, preferred_element_type=jnp.float32).astype(jnp.bfloat16)
        out_ref[0, :, c : c + HD] = both[:rows]
        out_ref[1, :, c : c + HD] = both[rows:]


def split_keys_values(kv):
    rows, _, channels = kv.shape
    return pl.pallas_call(
        split_body,
        out_shape=jax.ShapeDtypeStruct((2, rows, channels), jnp.bfloat16),
        in_specs=[vmem()],
        out_specs=vmem(),
        compiler_params=pltpu.CompilerParams(vmem_limit_bytes=SPLIT_VMEM),
        name="split_kv",
    )(kv)


def bias_body(tile_rows, mask_ref, out_ref):
    sign = 1 - 2 * (lax.axis_index("tile") % 2)
    for s, offset in enumerate(SLOTS):
        bit = mask_ref[0, WIN + sign * offset]
        block = jnp.full((tile_rows, LANES), jnp.where(bit > 0, 0.0, NEG), jnp.float32)
        out_ref[s * tile_rows : (s + 1) * tile_rows, :] = block


def mask_bias(mask, tile_rows):
    return pl.pallas_call(
        functools.partial(bias_body, tile_rows),
        out_shape=jax.ShapeDtypeStruct((len(SLOTS) * tile_rows, LANES), jnp.float32),
        in_specs=[smem()],
        out_specs=vmem(),
        compiler_params=pltpu.CompilerParams(vmem_limit_bytes=SPLIT_VMEM),
        name="mask_bias",
    )(mask)


def head_groups(count, channels):
    width = LANES // count * HD
    groups = [slice(c, min(c + width, channels)) for c in range(0, channels, width)]
    return groups, [(g.stop - g.start) // HD for g in groups]


def per_row(lanes, heads, count):
    return jnp.transpose(jnp.broadcast_to(lanes, (HD, heads * count)))


def attend_tiles(bias, src_ref, rows, gain_ref, tile_refs):
    count = rows.stop - rows.start
    groups, sizes = head_groups(count, src_ref.shape[1])
    x = src_ref[rows, :].astype(jnp.float32)
    inv = lax.rsqrt(jnp.mean(x * x, axis=-1, keepdims=True) + 1e-06)
    zero = jnp.zeros((count, HD), jnp.bfloat16)
    states = [src_ref[rows, g].astype(jnp.float32) for g in groups]
    queries = []
    for g, heads, state in zip(groups, sizes, states):
        query = (state * inv * gain_ref[:, g]).astype(jnp.bfloat16)
        blocks = [
            jnp.concatenate(
                [query[:, b * HD : (b + 1) * HD] if a == b else zero for b in range(heads)], axis=1
            )
            for a in range(heads)
        ]
        queries.append(jnp.concatenate(blocks, axis=0))
    scores = [
        lax.dot_general(
            jnp.concatenate([t[0, :, g] for t in tile_refs], axis=0),
            query,
            (((1,), (1,)), ((), ())),
            preferred_element_type=jnp.float32,
        )
        + bias[:, : heads * count]
        for g, heads, query in zip(groups, sizes, queries)
    ]
    tops = [jnp.max(s, axis=0, keepdims=True) for s in scores]

    def weigh(tops):
        weights = [jnp.exp2((s - top) * SCALE) for s, top in zip(scores, tops)]
        totals = [jnp.sum(w, axis=0, keepdims=True) for w in weights]
        mixed = [
            lax.dot_general(
                w.astype(jnp.bfloat16),
                jnp.concatenate([t[1, :, g] for t in tile_refs], axis=0),
                (((0,), (0,)), ((), ())),
                preferred_element_type=jnp.float32,
            )
            for g, w in zip(groups, weights)
        ]
        blocks = [
            [m[b * count : (b + 1) * count, b * HD : (b + 1) * HD] for b in range(heads)]
            for m, heads in zip(mixed, sizes)
        ]
        return totals, blocks

    return states, tops, weigh


def attend_rows(bias_ref, src_ref, rows, gain_ref, tile_refs):
    count = rows.stop - rows.start
    groups, sizes = head_groups(count, src_ref.shape[1])
    states, tops, weigh = attend_tiles(bias_ref[...], src_ref, rows, gain_ref, tile_refs)
    totals, mixed = weigh(tops)
    done = []
    for g, heads, state, blocks, total in zip(groups, sizes, states, mixed, totals):
        by_row = per_row(total, heads, count)
        parts = [m / by_row[b * count : (b + 1) * count] for b, m in enumerate(blocks)]
        done.append((g, state, jnp.concatenate(parts, axis=1).astype(jnp.bfloat16)))
    return done


def partial_body(slots, carried, last, bias_ref, src_ref, gain_ref, *refs):
    tile_refs = refs[: len(slots)]
    refs = refs[len(slots) :]
    top_in, total_in, sum_in = refs[:3] if carried else (None,) * 3
    refs = refs[3:] if carried else refs
    rows, channels = src_ref.shape
    tile_rows = tile_refs[0].shape[1]
    groups, sizes = head_groups(rows, channels)

    @pl.when(lax.axis_index("section") == 0)
    def _():
        bias = jnp.concatenate(
            [bias_ref[s * tile_rows : (s + 1) * tile_rows, :] for s in slots], axis=0
        )
        states, tops, weigh = attend_tiles(bias, src_ref, slice(0, rows), gain_ref, tile_refs)
        if carried:
            tops = [jnp.maximum(t, top_in[n : n + 1, :]) for n, t in enumerate(tops)]
        totals, sums = weigh(tops)
        for n, (g, heads) in enumerate(zip(groups, sizes)):
            total, blocks = totals[n], sums[n]
            if carried:
                fade = jnp.exp2((top_in[n : n + 1, :] - tops[n]) * SCALE)
                total = total + fade * total_in[n : n + 1, :]
                by_row = per_row(fade, heads, rows)
                blocks = [
                    m
                    + by_row[b * rows : (b + 1) * rows]
                    * sum_in[:, g.start + b * HD : g.start + (b + 1) * HD]
                    for b, m in enumerate(blocks)
                ]
            if not last:
                top_out, total_out, sum_out = refs
                top_out[n : n + 1, :] = tops[n]
                total_out[n : n + 1, :] = total
                for b, m in enumerate(blocks):
                    sum_out[:, g.start + b * HD : g.start + (b + 1) * HD] = m
                continue
            by_row = per_row(total, heads, rows)
            parts = [m / by_row[b * rows : (b + 1) * rows] for b, m in enumerate(blocks)]
            result = jnp.concatenate(parts, axis=1).astype(jnp.bfloat16)
            state = (states[n] + result.astype(jnp.float32)).astype(jnp.bfloat16)
            count = rows // PIECES
            for p in range(PIECES):
                span = slice(p * count, (p + 1) * count)
                refs[p][:, g] = result[span]
                refs[PIECES + p][:, g] = state[span]


def partial_attend(slots, last, bias, source, gain, tiles, carry=()):
    rows, channels = source.shape
    if last:
        piece = jax.ShapeDtypeStruct((rows // PIECES, channels), jnp.bfloat16)
        shapes = (piece,) * (2 * PIECES)
    else:
        lanes = jax.ShapeDtypeStruct((len(head_groups(rows, channels)[0]), LANES), jnp.float32)
        shapes = (lanes, lanes, jax.ShapeDtypeStruct((rows, channels), jnp.float32))
    operands = [bias, source, gain, *tiles, *carry]
    keys = len(tiles) * rows
    return pl.pallas_call(
        functools.partial(partial_body, slots, bool(carry), last),
        out_shape=shapes,
        in_specs=[vmem()] * len(operands),
        out_specs=(vmem(),) * len(shapes),
        compiler_params=pltpu.CompilerParams(vmem_limit_bytes=ATTEND_VMEM),
        cost_estimate=pl.CostEstimate(
            flops=4 * rows * keys * channels,
            bytes_accessed=4 * keys * channels + 6 * rows * channels,
            transcendentals=rows * keys * channels // HD,
        ),
        name="partial_attend",
    )(*operands)


def attend_body(moment, has_next, joined, bias_ref, src_ref, gain_ref, *refs):
    tile_refs = refs[: len(SLOTS)]
    rest = list(refs[len(SLOTS) :])
    kept_ref = rest.pop(0)
    earlier_refs = [rest.pop(0) for _ in range(joined)]
    out_ref = rest.pop(0)
    next_ref = rest.pop(0) if has_next else None
    live = lax.axis_index("section") == moment
    at = 0
    for ref in earlier_refs:
        out_ref[at : at + ref.shape[0], :] = ref[...]
        at += ref.shape[0]
    rows = src_ref.shape[0]
    span = slice(at, at + rows)

    @pl.when(live)
    def _():
        for g, state, result in attend_rows(bias_ref, src_ref, slice(0, rows), gain_ref, tile_refs):
            out_ref[span, g] = result
            if has_next:
                next_ref[:, g] = (state + result.astype(jnp.float32)).astype(jnp.bfloat16)

    @pl.when(jnp.logical_not(live))
    def _():
        out_ref[span, :] = kept_ref[...]


def attend(moment, has_next, bias, source, gain, tiles, kept, earlier):
    count, channels = source.shape
    keys = len(tiles) * tiles[0].shape[1]
    operands = [bias, source, gain, *tiles, kept, *earlier]
    total = count + sum(e.shape[0] for e in earlier)
    shapes = [jax.ShapeDtypeStruct((total, channels), jnp.bfloat16)]
    if has_next:
        shapes.append(jax.ShapeDtypeStruct((count, channels), jnp.bfloat16))
    return pl.pallas_call(
        functools.partial(attend_body, moment, has_next, len(earlier)),
        out_shape=tuple(shapes),
        in_specs=[vmem()] * len(operands),
        out_specs=(vmem(),) * len(shapes),
        compiler_params=pltpu.CompilerParams(vmem_limit_bytes=ATTEND_VMEM),
        cost_estimate=pl.CostEstimate(
            flops=4 * count * keys * channels,
            bytes_accessed=4 * keys * channels + 6 * count * channels,
            transcendentals=count * keys * channels // HD,
        ),
        name="attend",
    )(*operands)


def first_layer(raw, own, tiles, bias, hidden, gain):
    last = tiles - 1
    sections = lax.axis_size("section")

    def move(tile, pairs):
        return lax.ppermute(tile, ("section", "tile"), on_all(pairs))

    def on_all(pairs):
        return [
            (s * tiles + i, (s if i != j else (s ^ 1) % sections) * tiles + j)
            for s in range(sections)
            for i, j in pairs
        ]

    swap = [(i, i ^ 1) for i in range(tiles)]
    outward = [(0, 1), (last, last - 1)]
    outward += [(i, i + 2) for i in range(1, last, 2)] + [(i, i - 2) for i in range(2, tiles, 2)]
    relay = [(0, 0), (last, last)]
    relay += [(i, i + 1) for i in range(1, last, 2)] + [(i, i - 1) for i in range(2, tiles, 2)]
    first_raw = move(raw, outward)
    partner = move(own, swap)
    carry = partial_attend((0, 4), False, bias, hidden, gain, [own, partner])
    second = move(own, [(j, i) for i, j in outward])
    far_raw = move(first_raw, relay)
    first = split_keys_values(first_raw)
    partner_first = move(first, swap)
    partner_second = move(second, swap)
    tail = [first, second, partner_first, partner_second]
    carry = partial_attend((1, 2, 5, 6), False, bias, hidden, gain, tail, carry)
    far = split_keys_values(far_raw)
    pieces = partial_attend((3,), True, bias, hidden, gain, [far], carry)
    return [own, first, second, far, partner, partner_first, partner_second], pieces


def on_device(hidden, keys_values, q_gain, tile_mask):
    sections = lax.axis_size("section")
    rows = hidden.shape[0]
    raw = keys_values[0]
    own = split_keys_values(raw)
    bias = mask_bias(tile_mask, rows)
    window, pieces = first_layer(raw, own, lax.axis_size("tile"), bias, hidden, q_gain)
    kept, following = list(pieces[:PIECES]), list(pieces[PIECES:])
    for moment in range(1, sections):
        has_next = moment + 1 < sections
        others = [i for i in range(sections)[::-1] if i not in (moment - 1, moment)]
        cycle = [moment - 1, moment, *others]
        hop = list(zip(cycle, cycle[1:] + cycle[:1]))
        for p in range(PIECES):
            source = lax.ppermute(following[p], "section", hop)
            earlier = kept[:p] if not has_next and p + 1 == PIECES else ()
            results = attend(moment, has_next, bias, source, q_gain, window, kept[p], earlier)
            kept[p] = results[0]
            if has_next:
                following[p] = results[1]
    return kept[-1][None]


def solution(mesh):
    in_specs = (
        P("tile", None),
        P("section", "tile", None, None),
        P("section", None),
        P("tile", None),
    )
    out_specs = P("section", "tile", None)
    return jax.shard_map(
        on_device, mesh=mesh, in_specs=in_specs, out_specs=out_specs, check_vma=False
    )
```

```python
import functools

import jax
import jax.numpy as jnp
from jax import lax
from jax.experimental import pallas as pl
from jax.experimental.pallas import tpu as pltpu
from jax.sharding import PartitionSpec as P


HD = 128
WIN = 3
LANES = 128
NEG = -1e30
SCALE = HD**-0.5 * 1.4426950408889634
PIECES = 4
SLOTS = (0, 2, -2, -3, 1, -1, 3)
ATTEND_VMEM = 24 << 20
SPLIT_VMEM = 8 << 20


def vmem():
    return pl.BlockSpec(memory_space=pltpu.VMEM)


def smem():
    return pl.BlockSpec(memory_space=pltpu.SMEM)


def split_body(kv_ref, out_ref):
    rows = kv_ref.shape[0]
    i = lax.broadcasted_iota(jnp.int32, (2 * rows, 2 * rows), 0)
    j = lax.broadcasted_iota(jnp.int32, (2 * rows, 2 * rows), 1)
    source = jnp.where(i < rows, 2 * i, 2 * (i - rows) + 1)
    sort = jnp.where(j == source, 1.0, 0.0).astype(jnp.bfloat16)
    for c in range(0, kv_ref.shape[2], HD):
        mixed = kv_ref[:, :, c : c + HD].reshape(2 * rows, HD)
        both = jnp.dot(sort, mixed, preferred_element_type=jnp.float32).astype(jnp.bfloat16)
        out_ref[0, :, c : c + HD] = both[:rows]
        out_ref[1, :, c : c + HD] = both[rows:]


def split_keys_values(kv):
    rows, _, channels = kv.shape
    return pl.pallas_call(
        split_body,
        out_shape=jax.ShapeDtypeStruct((2, rows, channels), jnp.bfloat16),
        in_specs=[vmem()],
        out_specs=vmem(),
        compiler_params=pltpu.CompilerParams(vmem_limit_bytes=SPLIT_VMEM),
        name="split_kv",
    )(kv)


def bias_body(tile_rows, mask_ref, out_ref):
    sign = 1 - 2 * (lax.axis_index("tile") % 2)
    for s, offset in enumerate(SLOTS):
        bit = mask_ref[0, WIN + sign * offset]
        block = jnp.full((tile_rows, LANES), jnp.where(bit > 0, 0.0, NEG), jnp.float32)
        out_ref[s * tile_rows : (s + 1) * tile_rows, :] = block


def mask_bias(mask, tile_rows):
    return pl.pallas_call(
        functools.partial(bias_body, tile_rows),
        out_shape=jax.ShapeDtypeStruct((len(SLOTS) * tile_rows, LANES), jnp.float32),
        in_specs=[smem()],
        out_specs=vmem(),
        compiler_params=pltpu.CompilerParams(vmem_limit_bytes=SPLIT_VMEM),
        name="mask_bias",
    )(mask)


def head_groups(count, channels):
    width = LANES // count * HD
    groups = [slice(c, min(c + width, channels)) for c in range(0, channels, width)]
    return groups, [(g.stop - g.start) // HD for g in groups]


def per_row(lanes, heads, count):
    return jnp.transpose(jnp.broadcast_to(lanes, (HD, heads * count)))


def attend_tiles(bias, src_ref, rows, gain_ref, tile_refs):
    count = rows.stop - rows.start
    groups, sizes = head_groups(count, src_ref.shape[1])
    x = src_ref[rows, :].astype(jnp.float32)
    inv = lax.rsqrt(jnp.mean(x * x, axis=-1, keepdims=True) + 1e-06)
    zero = jnp.zeros((count, HD), jnp.bfloat16)
    states = [src_ref[rows, g].astype(jnp.float32) for g in groups]
    queries = []
    for g, heads, state in zip(groups, sizes, states):
        query = (state * inv * gain_ref[:, g]).astype(jnp.bfloat16)
        blocks = [
            jnp.concatenate(
                [query[:, b * HD : (b + 1) * HD] if a == b else zero for b in range(heads)], axis=1
            )
            for a in range(heads)
        ]
        queries.append(jnp.concatenate(blocks, axis=0))
    scores = [
        lax.dot_general(
            jnp.concatenate([t[0, :, g] for t in tile_refs], axis=0),
            query,
            (((1,), (1,)), ((), ())),
            preferred_element_type=jnp.float32,
        )
        + bias[:, : heads * count]
        for g, heads, query in zip(groups, sizes, queries)
    ]
    tops = [jnp.max(s, axis=0, keepdims=True) for s in scores]

    def weigh(tops):
        weights = [jnp.exp2((s - top) * SCALE) for s, top in zip(scores, tops)]
        totals = [jnp.sum(w, axis=0, keepdims=True) for w in weights]
        blocks = []
        for g, heads, w in zip(groups, sizes, weights):
            by_query = jnp.transpose(w.astype(jnp.bfloat16))
            parts = []
            for b in range(0, heads, 2):
                pair = slice(g.start + b * HD, g.start + (b + 2) * HD)
                both = jnp.dot(
                    by_query[b * count : (b + 2) * count],
                    jnp.concatenate([t[1, :, pair] for t in tile_refs], axis=0),
                    preferred_element_type=jnp.float32,
                )
                parts += [both[:count, :HD], both[count:, HD:]]
            blocks.append(parts)
        return totals, blocks

    return states, tops, weigh


def attend_rows(bias_ref, src_ref, rows, gain_ref, tile_refs):
    count = rows.stop - rows.start
    groups, sizes = head_groups(count, src_ref.shape[1])
    states, tops, weigh = attend_tiles(bias_ref[...], src_ref, rows, gain_ref, tile_refs)
    totals, mixed = weigh(tops)
    done = []
    for g, heads, state, blocks, total in zip(groups, sizes, states, mixed, totals):
        by_row = per_row(total, heads, count)
        parts = [m / by_row[b * count : (b + 1) * count] for b, m in enumerate(blocks)]
        done.append((g, state, jnp.concatenate(parts, axis=1).astype(jnp.bfloat16)))
    return done


def partial_body(slots, carried, last, bias_ref, src_ref, gain_ref, *refs):
    tile_refs = refs[: len(slots)]
    refs = refs[len(slots) :]
    top_in, total_in, sum_in = refs[:3] if carried else (None,) * 3
    refs = refs[3:] if carried else refs
    rows, channels = src_ref.shape
    tile_rows = tile_refs[0].shape[1]
    groups, sizes = head_groups(rows, channels)

    @pl.when(lax.axis_index("section") == 0)
    def _():
        bias = jnp.concatenate(
            [bias_ref[s * tile_rows : (s + 1) * tile_rows, :] for s in slots], axis=0
        )
        states, tops, weigh = attend_tiles(bias, src_ref, slice(0, rows), gain_ref, tile_refs)
        if carried:
            tops = [jnp.maximum(t, top_in[n : n + 1, :]) for n, t in enumerate(tops)]
        totals, sums = weigh(tops)
        for n, (g, heads) in enumerate(zip(groups, sizes)):
            total, blocks = totals[n], sums[n]
            if carried:
                fade = jnp.exp2((top_in[n : n + 1, :] - tops[n]) * SCALE)
                total = total + fade * total_in[n : n + 1, :]
                by_row = per_row(fade, heads, rows)
                blocks = [
                    m
                    + by_row[b * rows : (b + 1) * rows]
                    * sum_in[:, g.start + b * HD : g.start + (b + 1) * HD]
                    for b, m in enumerate(blocks)
                ]
            if not last:
                top_out, total_out, sum_out = refs
                top_out[n : n + 1, :] = tops[n]
                total_out[n : n + 1, :] = total
                for b, m in enumerate(blocks):
                    sum_out[:, g.start + b * HD : g.start + (b + 1) * HD] = m
                continue
            by_row = per_row(total, heads, rows)
            parts = [m / by_row[b * rows : (b + 1) * rows] for b, m in enumerate(blocks)]
            result = jnp.concatenate(parts, axis=1).astype(jnp.bfloat16)
            state = (states[n] + result.astype(jnp.float32)).astype(jnp.bfloat16)
            count = rows // PIECES
            for p in range(PIECES):
                span = slice(p * count, (p + 1) * count)
                refs[p][:, g] = result[span]
                refs[PIECES + p][:, g] = state[span]


def partial_attend(slots, last, bias, source, gain, tiles, carry=()):
    rows, channels = source.shape
    if last:
        piece = jax.ShapeDtypeStruct((rows // PIECES, channels), jnp.bfloat16)
        shapes = (piece,) * (2 * PIECES)
    else:
        lanes = jax.ShapeDtypeStruct((len(head_groups(rows, channels)[0]), LANES), jnp.float32)
        shapes = (lanes, lanes, jax.ShapeDtypeStruct((rows, channels), jnp.float32))
    operands = [bias, source, gain, *tiles, *carry]
    keys = len(tiles) * rows
    return pl.pallas_call(
        functools.partial(partial_body, slots, bool(carry), last),
        out_shape=shapes,
        in_specs=[vmem()] * len(operands),
        out_specs=(vmem(),) * len(shapes),
        compiler_params=pltpu.CompilerParams(vmem_limit_bytes=ATTEND_VMEM),
        cost_estimate=pl.CostEstimate(
            flops=4 * rows * keys * channels,
            bytes_accessed=4 * keys * channels + 6 * rows * channels,
            transcendentals=rows * keys * channels // HD,
        ),
        name="partial_attend",
    )(*operands)


def attend_body(moment, has_next, joined, bias_ref, src_ref, gain_ref, *refs):
    tile_refs = refs[: len(SLOTS)]
    rest = list(refs[len(SLOTS) :])
    kept_ref = rest.pop(0)
    earlier_refs = [rest.pop(0) for _ in range(joined)]
    out_ref = rest.pop(0)
    next_ref = rest.pop(0) if has_next else None
    live = lax.axis_index("section") == moment
    at = 0
    for ref in earlier_refs:
        out_ref[at : at + ref.shape[0], :] = ref[...]
        at += ref.shape[0]
    rows = src_ref.shape[0]
    span = slice(at, at + rows)

    @pl.when(live)
    def _():
        for g, state, result in attend_rows(bias_ref, src_ref, slice(0, rows), gain_ref, tile_refs):
            out_ref[span, g] = result
            if has_next:
                next_ref[:, g] = (state + result.astype(jnp.float32)).astype(jnp.bfloat16)

    @pl.when(jnp.logical_not(live))
    def _():
        out_ref[span, :] = kept_ref[...]


def attend(moment, has_next, bias, source, gain, tiles, kept, earlier):
    count, channels = source.shape
    keys = len(tiles) * tiles[0].shape[1]
    operands = [bias, source, gain, *tiles, kept, *earlier]
    total = count + sum(e.shape[0] for e in earlier)
    shapes = [jax.ShapeDtypeStruct((total, channels), jnp.bfloat16)]
    if has_next:
        shapes.append(jax.ShapeDtypeStruct((count, channels), jnp.bfloat16))
    return pl.pallas_call(
        functools.partial(attend_body, moment, has_next, len(earlier)),
        out_shape=tuple(shapes),
        in_specs=[vmem()] * len(operands),
        out_specs=(vmem(),) * len(shapes),
        compiler_params=pltpu.CompilerParams(vmem_limit_bytes=ATTEND_VMEM),
        cost_estimate=pl.CostEstimate(
            flops=4 * count * keys * channels,
            bytes_accessed=4 * keys * channels + 6 * count * channels,
            transcendentals=count * keys * channels // HD,
        ),
        name="attend",
    )(*operands)


def first_layer(raw, own, tiles, bias, hidden, gain):
    last = tiles - 1
    sections = lax.axis_size("section")

    def move(tile, pairs):
        return lax.ppermute(tile, ("section", "tile"), on_all(pairs))

    def on_all(pairs):
        return [
            (s * tiles + i, (s if i != j else (s ^ 1) % sections) * tiles + j)
            for s in range(sections)
            for i, j in pairs
        ]

    swap = [(i, i ^ 1) for i in range(tiles)]
    outward = [(0, 1), (last, last - 1)]
    outward += [(i, i + 2) for i in range(1, last, 2)] + [(i, i - 2) for i in range(2, tiles, 2)]
    relay = [(0, 0), (last, last)]
    relay += [(i, i + 1) for i in range(1, last, 2)] + [(i, i - 1) for i in range(2, tiles, 2)]
    first_raw = move(raw, outward)
    partner = move(own, swap)
    carry = partial_attend((0, 4), False, bias, hidden, gain, [own, partner])
    second = move(own, [(j, i) for i, j in outward])
    far_raw = move(first_raw, relay)
    first = split_keys_values(first_raw)
    partner_first = move(first, swap)
    partner_second = move(second, swap)
    tail = [first, second, partner_first, partner_second]
    carry = partial_attend((1, 2, 5, 6), False, bias, hidden, gain, tail, carry)
    far = split_keys_values(far_raw)
    pieces = partial_attend((3,), True, bias, hidden, gain, [far], carry)
    return [own, first, second, far, partner, partner_first, partner_second], pieces


def on_device(hidden, keys_values, q_gain, tile_mask):
    sections = lax.axis_size("section")
    rows = hidden.shape[0]
    raw = keys_values[0]
    own = split_keys_values(raw)
    bias = mask_bias(tile_mask, rows)
    window, pieces = first_layer(raw, own, lax.axis_size("tile"), bias, hidden, q_gain)
    kept, following = list(pieces[:PIECES]), list(pieces[PIECES:])
    for moment in range(1, sections):
        has_next = moment + 1 < sections
        others = [i for i in range(sections)[::-1] if i not in (moment - 1, moment)]
        cycle = [moment - 1, moment, *others]
        hop = list(zip(cycle, cycle[1:] + cycle[:1]))
        for p in range(PIECES):
            source = lax.ppermute(following[p], "section", hop)
            earlier = kept[:p] if not has_next and p + 1 == PIECES else ()
            results = attend(moment, has_next, bias, source, q_gain, window, kept[p], earlier)
            kept[p] = results[0]
            if has_next:
                following[p] = results[1]
    return kept[-1][None]


def solution(mesh):
    in_specs = (
        P("tile", None),
        P("section", "tile", None, None),
        P("section", None),
        P("tile", None),
    )
    out_specs = P("section", "tile", None)
    return jax.shard_map(
        on_device, mesh=mesh, in_specs=in_specs, out_specs=out_specs, check_vma=False
    )
```

```python
import functools

import jax
import jax.numpy as jnp
from jax import lax
from jax.experimental import pallas as pl
from jax.experimental.pallas import tpu as pltpu
from jax.sharding import PartitionSpec as P


HD = 128
WIN = 3
LANES = 128
NEG = -1e30
SCALE = HD**-0.5 * 1.4426950408889634
PIECES = 4
SLOTS = (0, 2, -2, -3, 1, -1, 3)
ATTEND_VMEM = 24 << 20
SPLIT_VMEM = 8 << 20


def vmem():
    return pl.BlockSpec(memory_space=pltpu.VMEM)


def smem():
    return pl.BlockSpec(memory_space=pltpu.SMEM)


def split_body(kv_ref, out_ref):
    rows = kv_ref.shape[0]
    i = lax.broadcasted_iota(jnp.int32, (2 * rows, 2 * rows), 0)
    j = lax.broadcasted_iota(jnp.int32, (2 * rows, 2 * rows), 1)
    source = jnp.where(i < rows, 2 * i, 2 * (i - rows) + 1)
    sort = jnp.where(j == source, 1.0, 0.0).astype(jnp.bfloat16)
    for c in range(0, kv_ref.shape[2], HD):
        mixed = kv_ref[:, :, c : c + HD].reshape(2 * rows, HD)
        both = jnp.dot(sort, mixed, preferred_element_type=jnp.float32).astype(jnp.bfloat16)
        out_ref[0, :, c : c + HD] = both[:rows]
        out_ref[1, :, c : c + HD] = both[rows:]


def split_keys_values(kv):
    rows, _, channels = kv.shape
    return pl.pallas_call(
        split_body,
        out_shape=jax.ShapeDtypeStruct((2, rows, channels), jnp.bfloat16),
        in_specs=[vmem()],
        out_specs=vmem(),
        compiler_params=pltpu.CompilerParams(vmem_limit_bytes=SPLIT_VMEM),
        name="split_kv",
    )(kv)


def bias_body(tile_rows, mask_ref, out_ref):
    sign = 1 - 2 * (lax.axis_index("tile") % 2)
    for s, offset in enumerate(SLOTS):
        bit = mask_ref[0, WIN + sign * offset]
        block = jnp.full((tile_rows, LANES), jnp.where(bit > 0, 0.0, NEG), jnp.float32)
        out_ref[s * tile_rows : (s + 1) * tile_rows, :] = block


def mask_bias(mask, tile_rows):
    return pl.pallas_call(
        functools.partial(bias_body, tile_rows),
        out_shape=jax.ShapeDtypeStruct((len(SLOTS) * tile_rows, LANES), jnp.float32),
        in_specs=[smem()],
        out_specs=vmem(),
        compiler_params=pltpu.CompilerParams(vmem_limit_bytes=SPLIT_VMEM),
        name="mask_bias",
    )(mask)


def head_groups(count, channels):
    width = LANES // count * HD
    groups = [slice(c, min(c + width, channels)) for c in range(0, channels, width)]
    return groups, [(g.stop - g.start) // HD for g in groups]


def per_row(lanes, heads, count):
    return jnp.transpose(jnp.broadcast_to(lanes, (HD, heads * count)))


def attend_tiles(bias, src_ref, rows, gain_ref, tile_refs):
    count = rows.stop - rows.start
    groups, sizes = head_groups(count, src_ref.shape[1])
    x = src_ref[rows, :].astype(jnp.float32)
    inv = lax.rsqrt(jnp.mean(x * x, axis=-1, keepdims=True) + 1e-06)
    zero = jnp.zeros((count, HD), jnp.bfloat16)
    states = [src_ref[rows, g].astype(jnp.float32) for g in groups]
    queries = []
    for g, heads, state in zip(groups, sizes, states):
        query = (state * inv * gain_ref[:, g]).astype(jnp.bfloat16)
        blocks = [
            jnp.concatenate(
                [query[:, b * HD : (b + 1) * HD] if a == b else zero for b in range(heads)], axis=1
            )
            for a in range(heads)
        ]
        queries.append(jnp.concatenate(blocks, axis=0))
    scores = [
        lax.dot_general(
            jnp.concatenate([t[0, :, g] for t in tile_refs], axis=0),
            query,
            (((1,), (1,)), ((), ())),
            preferred_element_type=jnp.float32,
        )
        + bias[:, : heads * count]
        for g, heads, query in zip(groups, sizes, queries)
    ]
    tops = [jnp.max(s, axis=0, keepdims=True) for s in scores]

    def weigh(tops):
        weights = [jnp.exp2((s - top) * SCALE) for s, top in zip(scores, tops)]
        totals = [jnp.sum(w, axis=0, keepdims=True) for w in weights]
        blocks = []
        for g, heads, w in zip(groups, sizes, weights):
            by_query = jnp.transpose(w.astype(jnp.bfloat16))
            parts = []
            for b in range(0, heads, 2):
                pair = slice(g.start + b * HD, g.start + (b + 2) * HD)
                both = jnp.dot(
                    by_query[b * count : (b + 2) * count],
                    jnp.concatenate([t[1, :, pair] for t in tile_refs], axis=0),
                    preferred_element_type=jnp.float32,
                )
                parts += [both[:count, :HD], both[count:, HD:]]
            blocks.append(parts)
        return totals, blocks

    return states, tops, weigh


def attend_rows(bias_ref, src_ref, rows, gain_ref, tile_refs):
    count = rows.stop - rows.start
    groups, sizes = head_groups(count, src_ref.shape[1])
    states, tops, weigh = attend_tiles(bias_ref[...], src_ref, rows, gain_ref, tile_refs)
    totals, mixed = weigh(tops)
    done = []
    for g, heads, state, blocks, total in zip(groups, sizes, states, mixed, totals):
        by_row = per_row(1.0 / total, heads, count)
        parts = [m * by_row[b * count : (b + 1) * count] for b, m in enumerate(blocks)]
        done.append((g, state, jnp.concatenate(parts, axis=1).astype(jnp.bfloat16)))
    return done


def partial_body(slots, carried, last, bias_ref, src_ref, gain_ref, *refs):
    tile_refs = refs[: len(slots)]
    refs = refs[len(slots) :]
    top_in, total_in, sum_in = refs[:3] if carried else (None,) * 3
    refs = refs[3:] if carried else refs
    rows, channels = src_ref.shape
    tile_rows = tile_refs[0].shape[1]
    groups, sizes = head_groups(rows, channels)

    @pl.when(lax.axis_index("section") == 0)
    def _():
        bias = jnp.concatenate(
            [bias_ref[s * tile_rows : (s + 1) * tile_rows, :] for s in slots], axis=0
        )
        states, tops, weigh = attend_tiles(bias, src_ref, slice(0, rows), gain_ref, tile_refs)
        if carried:
            tops = [jnp.maximum(t, top_in[n : n + 1, :]) for n, t in enumerate(tops)]
        totals, sums = weigh(tops)
        for n, (g, heads) in enumerate(zip(groups, sizes)):
            total, blocks = totals[n], sums[n]
            if carried:
                fade = jnp.exp2((top_in[n : n + 1, :] - tops[n]) * SCALE)
                total = total + fade * total_in[n : n + 1, :]
                by_row = per_row(fade, heads, rows)
                blocks = [
                    m
                    + by_row[b * rows : (b + 1) * rows]
                    * sum_in[:, g.start + b * HD : g.start + (b + 1) * HD]
                    for b, m in enumerate(blocks)
                ]
            if not last:
                top_out, total_out, sum_out = refs
                top_out[n : n + 1, :] = tops[n]
                total_out[n : n + 1, :] = total
                for b, m in enumerate(blocks):
                    sum_out[:, g.start + b * HD : g.start + (b + 1) * HD] = m
                continue
            by_row = per_row(1.0 / total, heads, rows)
            parts = [m * by_row[b * rows : (b + 1) * rows] for b, m in enumerate(blocks)]
            result = jnp.concatenate(parts, axis=1).astype(jnp.bfloat16)
            state = (states[n] + result.astype(jnp.float32)).astype(jnp.bfloat16)
            count = rows // PIECES
            for p in range(PIECES):
                span = slice(p * count, (p + 1) * count)
                refs[p][:, g] = result[span]
                refs[PIECES + p][:, g] = state[span]


def partial_attend(slots, last, bias, source, gain, tiles, carry=()):
    rows, channels = source.shape
    if last:
        piece = jax.ShapeDtypeStruct((rows // PIECES, channels), jnp.bfloat16)
        shapes = (piece,) * (2 * PIECES)
    else:
        lanes = jax.ShapeDtypeStruct((len(head_groups(rows, channels)[0]), LANES), jnp.float32)
        shapes = (lanes, lanes, jax.ShapeDtypeStruct((rows, channels), jnp.float32))
    operands = [bias, source, gain, *tiles, *carry]
    keys = len(tiles) * rows
    return pl.pallas_call(
        functools.partial(partial_body, slots, bool(carry), last),
        out_shape=shapes,
        in_specs=[vmem()] * len(operands),
        out_specs=(vmem(),) * len(shapes),
        compiler_params=pltpu.CompilerParams(vmem_limit_bytes=ATTEND_VMEM),
        cost_estimate=pl.CostEstimate(
            flops=4 * rows * keys * channels,
            bytes_accessed=4 * keys * channels + 6 * rows * channels,
            transcendentals=rows * keys * channels // HD,
        ),
        name="partial_attend",
    )(*operands)


def attend_body(moment, has_next, joined, bias_ref, src_ref, gain_ref, *refs):
    tile_refs = refs[: len(SLOTS)]
    rest = list(refs[len(SLOTS) :])
    kept_ref = rest.pop(0)
    earlier_refs = [rest.pop(0) for _ in range(joined)]
    out_ref = rest.pop(0)
    next_ref = rest.pop(0) if has_next else None
    live = lax.axis_index("section") == moment
    at = 0
    for ref in earlier_refs:
        out_ref[at : at + ref.shape[0], :] = ref[...]
        at += ref.shape[0]
    rows = src_ref.shape[0]
    span = slice(at, at + rows)

    @pl.when(live)
    def _():
        for g, state, result in attend_rows(bias_ref, src_ref, slice(0, rows), gain_ref, tile_refs):
            out_ref[span, g] = result
            if has_next:
                next_ref[:, g] = (state + result.astype(jnp.float32)).astype(jnp.bfloat16)

    @pl.when(jnp.logical_not(live))
    def _():
        out_ref[span, :] = kept_ref[...]


def attend(moment, has_next, bias, source, gain, tiles, kept, earlier):
    count, channels = source.shape
    keys = len(tiles) * tiles[0].shape[1]
    operands = [bias, source, gain, *tiles, kept, *earlier]
    total = count + sum(e.shape[0] for e in earlier)
    shapes = [jax.ShapeDtypeStruct((total, channels), jnp.bfloat16)]
    if has_next:
        shapes.append(jax.ShapeDtypeStruct((count, channels), jnp.bfloat16))
    return pl.pallas_call(
        functools.partial(attend_body, moment, has_next, len(earlier)),
        out_shape=tuple(shapes),
        in_specs=[vmem()] * len(operands),
        out_specs=(vmem(),) * len(shapes),
        compiler_params=pltpu.CompilerParams(vmem_limit_bytes=ATTEND_VMEM),
        cost_estimate=pl.CostEstimate(
            flops=4 * count * keys * channels,
            bytes_accessed=4 * keys * channels + 6 * count * channels,
            transcendentals=count * keys * channels // HD,
        ),
        name="attend",
    )(*operands)


def first_layer(raw, own, tiles, bias, hidden, gain):
    last = tiles - 1
    sections = lax.axis_size("section")

    def move(tile, pairs):
        return lax.ppermute(tile, ("section", "tile"), on_all(pairs))

    def on_all(pairs):
        return [
            (s * tiles + i, (s if i != j else (s ^ 1) % sections) * tiles + j)
            for s in range(sections)
            for i, j in pairs
        ]

    swap = [(i, i ^ 1) for i in range(tiles)]
    outward = [(0, 1), (last, last - 1)]
    outward += [(i, i + 2) for i in range(1, last, 2)] + [(i, i - 2) for i in range(2, tiles, 2)]
    relay = [(0, 0), (last, last)]
    relay += [(i, i + 1) for i in range(1, last, 2)] + [(i, i - 1) for i in range(2, tiles, 2)]
    first_raw = move(raw, outward)
    partner = move(own, swap)
    carry = partial_attend((0, 4), False, bias, hidden, gain, [own, partner])
    second = move(own, [(j, i) for i, j in outward])
    far_raw = move(first_raw, relay)
    first = split_keys_values(first_raw)
    partner_first = move(first, swap)
    partner_second = move(second, swap)
    tail = [first, second, partner_first, partner_second]
    carry = partial_attend((1, 2, 5, 6), False, bias, hidden, gain, tail, carry)
    far = split_keys_values(far_raw)
    pieces = partial_attend((3,), True, bias, hidden, gain, [far], carry)
    return [own, first, second, far, partner, partner_first, partner_second], pieces


def on_device(hidden, keys_values, q_gain, tile_mask):
    sections = lax.axis_size("section")
    rows = hidden.shape[0]
    raw = keys_values[0]
    own = split_keys_values(raw)
    bias = mask_bias(tile_mask, rows)
    window, pieces = first_layer(raw, own, lax.axis_size("tile"), bias, hidden, q_gain)
    kept, following = list(pieces[:PIECES]), list(pieces[PIECES:])
    for moment in range(1, sections):
        has_next = moment + 1 < sections
        others = [i for i in range(sections)[::-1] if i not in (moment - 1, moment)]
        cycle = [moment - 1, moment, *others]
        hop = list(zip(cycle, cycle[1:] + cycle[:1]))
        for p in range(PIECES):
            source = lax.ppermute(following[p], "section", hop)
            earlier = kept[:p] if not has_next and p + 1 == PIECES else ()
            results = attend(moment, has_next, bias, source, q_gain, window, kept[p], earlier)
            kept[p] = results[0]
            if has_next:
                following[p] = results[1]
    return kept[-1][None]


def solution(mesh):
    in_specs = (
        P("tile", None),
        P("section", "tile", None, None),
        P("section", None),
        P("tile", None),
    )
    out_specs = P("section", "tile", None)
    return jax.shard_map(
        on_device, mesh=mesh, in_specs=in_specs, out_specs=out_specs, check_vma=False
    )
```
